32 devices in a mesh: groups: 2 (over y), cand: 4 (over z), tensor: 4 (over x, core).
Axes of the slice: x: 2, y: 2, z: 4, core: 2. Of those that a mesh axis runs over, the one named last changes fastest.
Arguments:
- response_latest_embeddings: bfloat16 [16, 384, 8192], P(('groups', 'cand'), None, 'tensor'), parts along dimension 0, may hold values from -6 to 6
- critic_probe_projector: bfloat16 [8192, 4096], P('cand', 'tensor'), may hold values from -0.0625 to 0.0625
- critic_pair_projector: bfloat16 [8192, 2048], P('cand', 'tensor'), may hold values from -0.0625 to 0.0625
- critic_stored_pairs: bfloat16 [16, 2048, 2048], P(('groups', 'cand'), None, 'tensor'), parts along dimension 0, may hold values from -1000 to 1000
- critic_grading_vector: float32 [4096], P('tensor'), may hold values from -6 to 6
- actor_stored_pairs: bfloat16 [16, 2048, 8, 256], P(('groups', 'cand'), None, 'tensor'), parts along dimension 0, may hold values from -1000 to 1000
- filled_extents: int32 [16], P('groups'), parts along dimension 0, may hold values from 1 to 2048, as said below
- kept_responses: int32 [8], P('groups'), parts along dimension 0, may hold values from 0 to 7, as said below
- actor_latest_probes: bfloat16 [8, 4, 4096], P(('groups', 'cand'), None, 'tensor'), parts along dimension 0, may hold values from -6 to 6
- actor_latest_pairs: bfloat16 [8, 4, 2048], P(('groups', 'cand'), None, 'tensor'), parts along dimension 0, may hold values from -6 to 6
Outputs:
- token_rewards: float32 [16, 384], P(('groups', 'cand')), parts along dimension 0
- actor_mixing_result: bfloat16 [8, 4, 4096], P(('groups', 'cand'), None, 'tensor'), parts along dimension 0
The draws below stay inside these ranges and needn't reach their ends.
There are 2 independent parts, one for each index of `groups`. The reference program is written for one: setup_inputs(seed, part) draws one part's arguments, and reference() takes and returns one part's arrays. A program takes and returns all parts, laid end to end along the dimension named above; an argument that names none is the same for every part. Nothing has to cross between parts.
Inputs may be any that keep to these rules, and one draw needn't show every extreme that they name: `kept_responses`: distinct candidate ids, always including 0 and 7. `filled_extents`: some candidate has exactly 2048 live tokens.
All inputs are finite; a program needn't handle non-finite values.
Results may differ from the reference program's by a relative error of at most 0.012.
The reference program's roundings to bfloat16 on the way count: a program that leaves them out, or rounds other values in their place, can miss the bound.
Values may be sent and summed in bfloat16 or wider, within the bound.
A program may use at most 128 MiB of HBM per device.

```python
import jax
import jax.numpy as jnp
from jax import lax

D = 8192
RQH = 32
RKV = 8
HD = 128
PQH = 32
PKV = 8
CTX = 2048
SPAN = 384
PMAX = 2048
NEW = 4
CANDS = 8
KEEP = 4


def cache_entries(key, cands, length, heads):
    base = jnp.clip(jax.random.normal(key, (cands, length, heads, 2 * HD), jnp.float32), -6.0, 6.0)
    return base


def draw_critic_stored_pairs(key, part):
    values = cache_entries(jax.random.fold_in(key, 21), CANDS, CTX, RKV)
    return values.reshape(CANDS, CTX, RKV * 2 * HD).astype(jnp.bfloat16)


def draw_actor_stored_pairs(key, part):
    return cache_entries(jax.random.fold_in(key, 23), CANDS, PMAX, PKV).astype(jnp.bfloat16)


def draw_filled_extents(key, part):
    key_one, key_two = jax.random.split(jax.random.fold_in(key, 11))
    values = jax.random.randint(key_one, (CANDS,), 1, PMAX + 1)
    full_at = jax.random.randint(key_two, (), 0, CANDS)
    return values.at[full_at].set(PMAX).astype(jnp.int32)


def draw_kept_responses(key, part):
    key_one, key_two = jax.random.split(jax.random.fold_in(key, 13))
    middle = jax.random.permutation(key_one, jnp.arange(1, CANDS - 1, dtype=jnp.int32))[:KEEP - 2]
    chosen_lanes = jnp.concatenate([jnp.array([0, CANDS - 1], jnp.int32), middle])
    return jax.random.permutation(key_two, chosen_lanes).astype(jnp.int32)


def steps_of(rng, extent, cuts, smallest, top_value):
    def one(dim, parts):
        steps = jax.random.uniform(jax.random.fold_in(jax.random.fold_in(rng, 6), dim), (parts,), jnp.float32, smallest / len(cuts), top_value / len(cuts))
        return jnp.repeat(jnp.exp(steps), extent[dim] // parts).reshape((-1,) + (1,) * (len(extent) - dim - 1))

    loudness = one(*cuts[0])
    for cut in cuts[1:]:
        loudness = loudness * one(*cut)
    return loudness


def scatter_about(stream_key, dims, spread, most, cuts=(), kind=jnp.bfloat16):
    values = jax.random.normal(stream_key, dims, jnp.float32) * spread
    if len(cuts) > 0:
        values = steps_of(stream_key, dims, cuts, -0.22, 0.18) * values
    return jnp.clip(values, min=-most, max=most).astype(kind)


def setup_inputs(seed: int = 0, part: int = 0) -> dict:
    splits = jax.random.split(jax.random.key(seed), 11)
    part_keys = jax.random.split(jax.random.fold_in(splits[10], part), 11)
    return {
        "response_latest_embeddings": scatter_about(part_keys[0], (CANDS, SPAN, D), 1.0, 6.0, ((0, 4), (2, 4))),
        "critic_probe_projector": scatter_about(splits[1], (D, RQH * HD), D ** -0.5, 0.0625, ((0, 4), (1, 4))),
        "critic_pair_projector": scatter_about(splits[2], (D, RKV * 2 * HD), D ** -0.5, 0.0625, ((0, 4), (1, 4))),
        "critic_stored_pairs": draw_critic_stored_pairs(jax.random.fold_in(jax.random.fold_in(splits[10], part), 71), part),
        "critic_grading_vector": scatter_about(splits[4], (RQH * HD,), 1.0, 6.0, ((0, 4),), jnp.float32),
        "actor_stored_pairs": draw_actor_stored_pairs(jax.random.fold_in(jax.random.fold_in(splits[10], part), 71), part),
        "filled_extents": draw_filled_extents(jax.random.fold_in(jax.random.fold_in(splits[10], part), 71), part),
        "kept_responses": draw_kept_responses(jax.random.fold_in(jax.random.fold_in(splits[10], part), 71), part),
        "actor_latest_probes": scatter_about(part_keys[8], (KEEP, NEW, PQH * HD), 1.0, 6.0, ((0, 4), (2, 4))),
        "actor_latest_pairs": scatter_about(part_keys[9], (KEEP, NEW, PKV * 2 * HD), 1.0, 6.0, ((0, 4), (2, 4))),
    }


masked_value = -1e30


def reference(response_latest_embeddings, critic_probe_projector, critic_pair_projector, critic_stored_pairs, critic_grading_vector, actor_stored_pairs, filled_extents, kept_responses, actor_latest_probes, actor_latest_pairs):
    tok_rows = response_latest_embeddings.reshape(CANDS * SPAN, D)
    query_heads = jnp.dot(tok_rows, critic_probe_projector, preferred_element_type=jnp.float32).astype(jnp.bfloat16)
    keyval = jnp.dot(tok_rows, critic_pair_projector, preferred_element_type=jnp.float32).astype(jnp.bfloat16)
    query_heads = query_heads.reshape(CANDS, SPAN, RKV, RQH // RKV, HD)
    keyval = keyval.reshape(CANDS, SPAN, RKV, 2 * HD)
    cached = critic_stored_pairs.reshape(CANDS, CTX, RKV, 2 * HD)
    causal = jnp.arange(SPAN)[:, None] >= jnp.arange(SPAN)[None, :]
    visible = jnp.concatenate([jnp.ones((SPAN, CTX), dtype=bool), causal], axis=1)

    def score_one(entry_pair):
        queries, fresh_keys, old_keys = entry_pair
        every_key = jnp.concatenate([old_keys, fresh_keys], axis=0).astype(jnp.float32)
        scores = jnp.einsum("tkgd,skd->kgts", queries.astype(jnp.float32), every_key[..., :HD]) * HD ** -0.5
        scores = jnp.where(visible, scores, masked_value)
        rounded = lax.optimization_barrier(jax.nn.softmax(scores, axis=-1).astype(jnp.bfloat16))
        heads_out = jnp.einsum("kgts,skd->tkgd", rounded.astype(jnp.float32), every_key[..., HD:])
        return jnp.dot(heads_out.reshape(SPAN, RQH * HD), critic_grading_vector, precision=lax.Precision.HIGHEST)

    token_rewards = lax.map(score_one, (query_heads, keyval, cached))

    causal_new = jnp.arange(NEW)[:, None] >= jnp.arange(NEW)[None, :]

    def generate_for_lane(entry_pair):
        chosen_lanes, queries, fresh_keys = entry_pair
        old_keys = lax.dynamic_index_in_dim(actor_stored_pairs, chosen_lanes, 0, keepdims=False)
        live_len = lax.dynamic_index_in_dim(filled_extents, chosen_lanes, 0, keepdims=False)
        living_response_flags = jnp.arange(PMAX) < live_len
        visible_new = jnp.concatenate([jnp.broadcast_to(living_response_flags, (NEW, PMAX)), causal_new], axis=1)
        every_key = jnp.concatenate([old_keys, fresh_keys.reshape(NEW, PKV, 2 * HD)], axis=0).astype(jnp.float32)
        heads_in = queries.reshape(NEW, PKV, PQH // PKV, HD).astype(jnp.float32)
        scores = jnp.einsum("ikgd,skd->kgis", heads_in, every_key[..., :HD]) * HD ** -0.5
        scores = jnp.where(visible_new, scores, masked_value)
        weights = jax.nn.softmax(scores, axis=-1)
        heads_out = jnp.einsum("kgis,skd->ikgd", weights, every_key[..., HD:])
        return heads_out.reshape(NEW, PQH * HD).astype(jnp.bfloat16)

    actor_mixing_result = lax.map(generate_for_lane, (kept_responses, actor_latest_probes, actor_latest_pairs))
    return token_rewards, actor_mixing_result
```

```python
import functools

import jax
import jax.numpy as jnp
from jax import lax
from jax.experimental import pallas as pl
from jax.experimental.pallas import tpu as pltpu
from jax.sharding import PartitionSpec as P

HD = 128
CW = 2 * HD
AHEAD = 2
MESH = pl.DeviceIdType.MESH

masked_value = -1e30


def project_kernel(
    nz, nt, per_group,
    x_ref, wq_ref, wkv_ref, cache_ref, grade_ref, out_ref,
    xbuf, wbuf, cbuf, acts,
    load_sem, right_sem, left_sem, line_sem, pair_send, pair_recv,
    x_right, x_left, x_line, x_pair_send, x_pair_recv,
):
    nchunk, depth, _ = wbuf.shape
    dz = depth // nz
    half = dz // 2
    nx = nt // 2
    cands, span, _ = out_ref.shape
    context = cbuf.shape[1]
    qchunks = per_group * HD // CW
    stride = 1 + qchunks
    y = lax.axis_index("groups")
    z = lax.axis_index("cand")
    t = lax.axis_index("tensor")
    x = t // 2
    c = t - 2 * x

    loads = []
    for k in range(nchunk):
        g, j = k // stride, k % stride
        if j == 0:
            src = wkv_ref.at[:, pl.ds(g * CW, CW)]
        else:
            src = wq_ref.at[:, pl.ds((g * qchunks + j - 1) * CW, CW)]
        loads.append(
            pltpu.make_async_copy(
                src, wbuf.at[k, pl.ds(pl.multiple_of(z * dz, dz), dz), :], load_sem.at[k]
            )
        )
    x_load = pltpu.make_async_copy(x_ref, xbuf.at[t], load_sem.at[nchunk])
    c_load = pltpu.make_async_copy(cache_ref, cbuf, load_sem.at[nchunk + 1])
    for k in range(min(AHEAD, nchunk)):
        loads[k].start()
    x_load.start()
    for k in range(min(AHEAD, nchunk), nchunk):
        loads[k].start()
    c_load.start()

    barrier = pltpu.get_barrier_semaphore()

    def greet(device):
        pl.semaphore_signal(barrier, inc=1, device_id=device, device_id_type=MESH)

    greet({"groups": 1 - y})
    greet({"tensor": 2 * x + 1 - c})

    @pl.when(z > 0)
    def _():
        greet({"cand": z - 1})

    @pl.when(z < nz - 1)
    def _():
        greet({"cand": z + 1})

    @pl.when(x > 0)
    def _():
        greet({"tensor": t - 2})

    @pl.when(x < nx - 1)
    def _():
        greet({"tensor": t + 2})

    ends = [z > 0, z < nz - 1, x > 0, x < nx - 1]
    pl.semaphore_wait(barrier, 2 + sum(e.astype(jnp.int32) for e in ends))

    def remote(ref, send, recv, device):
        return pltpu.make_async_remote_copy(
            src_ref=ref, dst_ref=ref, send_sem=send, recv_sem=recv,
            device_id=device, device_id_type=MESH,
        )

    def piece(k, o, side):
        return wbuf.at[k, pl.ds(pl.multiple_of(o * dz + side * half, half), half), :]

    def go_right(k, o):
        return remote(piece(k, o, y), right_sem.at[k, o], line_sem.at[k, o], {"cand": z + 1})

    def go_left(k, o):
        return remote(piece(k, o, y), left_sem.at[k, o], line_sem.at[k, o], {"cand": z - 1})

    def to_pair(k, o):
        return remote(piece(k, o, y), pair_send.at[k, o], pair_recv.at[k, o], {"groups": 1 - y})

    def from_pair(k, o):
        return remote(piece(k, o, 1 - y), pair_send.at[k, o], pair_recv.at[k, o], {"groups": 1 - y})

    def send_own(k):
        @pl.when(z < nz - 1)
        def _():
            go_right(k, z).start()

        @pl.when(z > 0)
        def _():
            go_left(k, z).start()

    def x_go_right(o):
        return remote(xbuf.at[2 * o + c], x_right.at[o], x_line.at[o], {"tensor": t + 2})

    def x_go_left(o):
        return remote(xbuf.at[2 * o + c], x_left.at[o], x_line.at[o], {"tensor": t - 2})

    def x_to_pair(o):
        return remote(xbuf.at[2 * o + c], x_pair_send.at[o], x_pair_recv.at[o], {"tensor": 2 * x + 1 - c})

    def x_from_pair(o):
        return remote(xbuf.at[2 * o + 1 - c], x_pair_send.at[o], x_pair_recv.at[o], {"tensor": 2 * x + 1 - c})

    for k in range(min(AHEAD, nchunk)):
        loads[k].wait()
        send_own(k)
    x_load.wait()

    @pl.when(x < nx - 1)
    def _():
        x_go_right(x).start()

    @pl.when(x > 0)
    def _():
        x_go_left(x).start()

    x_to_pair(x).start()
    for k in range(min(AHEAD, nchunk), nchunk):
        loads[k].wait()
    c_load.wait()
    out_ref[...] = jnp.zeros_like(out_ref)

    def finish_x():
        for d in range(1, nx):
            @pl.when(x - d >= 0)
            def _(d=d):
                x_go_right(x - d).wait_recv()
                x_to_pair(x - d).start()

                @pl.when(x < nx - 1)
                def _():
                    x_go_right(x - d).start()

            @pl.when(x + d < nx)
            def _(d=d):
                x_go_left(x + d).wait_recv()
                x_to_pair(x + d).start()

                @pl.when(x > 0)
                def _():
                    x_go_left(x + d).start()

        for o in range(nx):
            x_from_pair(o).wait_recv()

    def relay(k):
        def one(d, carry):
            @pl.when(z - d >= 0)
            def _():
                o = z - d
                go_right(k, o).wait_recv()

                @pl.when(z < nz - 1)
                def _():
                    go_right(k, o).start()

                to_pair(k, o).start()

            @pl.when(z + d < nz)
            def _():
                o = z + d
                go_left(k, o).wait_recv()

                @pl.when(z > 0)
                def _():
                    go_left(k, o).start()

                to_pair(k, o).start()

            return carry

        lax.fori_loop(1, nz, one, 0)

    rows = cands * span
    dx = depth // nt
    row_tile = rows // 3

    def attend(k):
        g = k // stride
        base = pl.multiple_of(g * CW, CW)
        kv_at = g * stride
        ri = lax.broadcasted_iota(jnp.int32, (span, span), 0)
        ci = lax.broadcasted_iota(jnp.int32, (span, span), 1)
        head0 = (g * qchunks + (k - kv_at) - 1) * 2

        def one(b, carry):
            at = pl.ds(pl.multiple_of(b * span, span), span)
            old_k = cbuf[b, :, pl.ds(base, HD)]
            old_v = cbuf[b, :, pl.ds(pl.multiple_of(base + HD, HD), HD)]
            new_k = acts[kv_at, at, :HD]
            new_v = acts[kv_at, at, HD:]
            for h in range(2):
                q = acts[k, at, h * HD:(h + 1) * HD]
                dims = (((1,), (1,)), ((), ()))
                s1 = lax.dot_general(q, old_k, dims, preferred_element_type=jnp.float32)
                s2 = lax.dot_general(q, new_k, dims, preferred_element_type=jnp.float32)
                s2 = jnp.where(ri >= ci, s2, masked_value)
                top = jnp.maximum(
                    jnp.max(s1, axis=1, keepdims=True), jnp.max(s2, axis=1, keepdims=True)
                )
                scale = HD ** -0.5
                e1 = jnp.exp((s1 - top) * scale)
                e2 = jnp.exp((s2 - top) * scale)
                total = jnp.sum(e1, axis=1, keepdims=True) + jnp.sum(e2, axis=1, keepdims=True)
                o = jnp.dot(e1.astype(jnp.bfloat16), old_v, preferred_element_type=jnp.float32)
                o = o + jnp.dot(e2.astype(jnp.bfloat16), new_v, preferred_element_type=jnp.float32)
                weight = grade_ref[pl.ds(head0 + h, 1), :]
                out_ref[b] += (o / total) * weight
            return carry

        lax.fori_loop(0, cands, one, 0)

    def compute(k):
        def take(d, carry):
            o = jnp.where(d < z, d, d + 1)
            from_pair(k, o).wait_recv()
            return carry

        lax.fori_loop(0, nz - 1, take, 0)

        def tile(r, carry):
            at = pl.ds(pl.multiple_of(r * row_tile, row_tile), row_tile)
            acc = jnp.zeros((row_tile, CW), jnp.float32)
            for s in range(nt):
                acc = acc + jnp.dot(
                    xbuf[s, at, :], wbuf[k, s * dx:(s + 1) * dx, :],
                    preferred_element_type=jnp.float32,
                )
            acts[k, at, :] = acc.astype(jnp.bfloat16)
            return carry

        lax.fori_loop(0, rows // row_tile, tile, 0)

        @pl.when(k % stride != 0)
        def _():
            attend(k)

    def done(k):
        return jnp.maximum(0, jnp.minimum(k, 2 * (k - 2)))

    def step(k, carry):
        @pl.when(k + AHEAD < nchunk)
        def _():
            send_own(k + AHEAD)

        relay(k)

        @pl.when(k == min(2, nchunk - 1))
        def _():
            finish_x()

        def inner(j, c2):
            compute(j)
            return c2

        last = jnp.where(k == nchunk - 1, nchunk, done(k))
        lax.fori_loop(done(k - 1), last, inner, 0)
        return carry

    lax.fori_loop(0, nchunk, step, 0)

    def drain(k, carry):
        def one(o, c2):
            @pl.when((o <= z) & (z < nz - 1))
            def _():
                go_right(k, o).wait_send()

            @pl.when((o >= z) & (z > 0))
            def _():
                go_left(k, o).wait_send()

            @pl.when(o != z)
            def _():
                to_pair(k, o).wait_send()

            return c2

        lax.fori_loop(0, nz, one, 0)
        return carry

    lax.fori_loop(0, nchunk, drain, 0)
    for o in range(nx):
        x_to_pair(o).wait_send()

        @pl.when((o <= x) & (x < nx - 1))
        def _(o=o):
            x_go_right(o).wait_send()

        @pl.when((o >= x) & (x > 0))
        def _(o=o):
            x_go_left(o).wait_send()


def reward_partial(nz, nt, x, wq, wkv, cache, grade):
    cands, span, dx = x.shape
    rows = cands * span
    depth = wq.shape[0] * nz
    groups_here = wkv.shape[1] // CW
    per_group = wq.shape[1] // HD // groups_here
    nchunk = (wq.shape[1] + wkv.shape[1]) // CW
    dma = pltpu.SemaphoreType.DMA
    nx = nt // 2
    anywhere = pl.BlockSpec(memory_space=pl.ANY)
    return pl.pallas_call(
        functools.partial(project_kernel, nz, nt, per_group),
        out_shape=jax.ShapeDtypeStruct((cands, span, HD), jnp.float32),
        in_specs=[anywhere] * 4 + [pl.BlockSpec(memory_space=pltpu.VMEM)],
        out_specs=pl.BlockSpec(memory_space=pltpu.VMEM),
        scratch_shapes=[
            pltpu.VMEM((nt, rows, dx), jnp.bfloat16),
            pltpu.VMEM((nchunk, depth, CW), jnp.bfloat16),
            pltpu.VMEM(cache.shape, jnp.bfloat16),
            pltpu.VMEM((nchunk, rows, CW), jnp.bfloat16),
            dma((nchunk + 2,)),
            dma((nchunk, nz)), dma((nchunk, nz)), dma((nchunk, nz)),
            dma((nchunk, nz)), dma((nchunk, nz)),
            dma((nx,)), dma((nx,)), dma((nx,)), dma((nx,)), dma((nx,)),
        ],
        compiler_params=pltpu.CompilerParams(
            collective_id=0, has_side_effects=True, vmem_limit_bytes=67043328
        ),
    )(x.reshape(rows, dx), wq, wkv, cache, grade.reshape(-1, HD))


def policy(
    cand_here, actor_stored_pairs, filled_extents, kept_responses, actor_latest_probes, actor_latest_pairs
):
    key_scale = HD ** (-0.5)
    device_here = lax.axis_index("cand")
    lane_number = kept_responses.shape[0]
    new_count = actor_latest_probes.shape[1]
    kv_here = actor_stored_pairs.shape[2]
    policy_heads = actor_latest_probes.shape[2] // HD
    policy_group = policy_heads // kv_here
    cache_len = actor_stored_pairs.shape[1]
    causal_new = lax.broadcasted_iota(jnp.int32, (new_count, new_count), 0) >= lax.broadcasted_iota(
        jnp.int32, (new_count, new_count), 1
    )
    both = lax.all_gather(
        jnp.concatenate([actor_latest_probes, actor_latest_pairs], axis=2), "cand", axis=0, tiled=True
    )
    all_queries = both[..., : policy_heads * HD]
    all_fresh = both[..., policy_heads * HD:]
    ids_here = device_here * cand_here + lax.broadcasted_iota(jnp.int32, (cand_here,), 0)
    matched = kept_responses[None, :] == ids_here[:, None]
    slot_index = jnp.sum(
        jnp.where(matched, lax.broadcasted_iota(jnp.int32, (cand_here, lane_number), 1), 0), axis=1
    )
    own_queries = jnp.take(all_queries, slot_index, axis=0).reshape(
        cand_here, new_count, kv_here, policy_group, HD
    )
    own_fresh = jnp.take(all_fresh, slot_index, axis=0).reshape(
        cand_here, new_count, kv_here, 2 * HD
    )
    sequence_places = lax.broadcasted_iota(jnp.int32, (cache_len,), 0)
    living = sequence_places[None, :] < jnp.take(filled_extents, ids_here)[:, None]
    living = living[:, None, None, None, :]
    scores = (
        jnp.einsum(
            "cikgd,ctkd->ckgit", own_queries, actor_stored_pairs[..., :HD],
            preferred_element_type=jnp.float32,
        )
        * key_scale
    )
    scores = jnp.where(living, scores, masked_value)
    fresh_scores = (
        jnp.einsum(
            "cikgd,cjkd->ckgij", own_queries, own_fresh[..., :HD], preferred_element_type=jnp.float32
        )
        * key_scale
    )
    fresh_scores = jnp.where(causal_new, fresh_scores, masked_value)
    peak = jnp.maximum(jnp.max(scores, axis=-1), jnp.max(fresh_scores, axis=-1))
    old_weights = jnp.where(living, jnp.exp(scores - peak[..., None]), 0.0)
    fresh_weights = jnp.where(causal_new, jnp.exp(fresh_scores - peak[..., None]), 0.0)
    denominator = jnp.sum(old_weights, axis=-1) + jnp.sum(fresh_weights, axis=-1)
    numerator = jnp.einsum(
        "ckgit,ctkd->ckgid", old_weights, actor_stored_pairs[..., HD:],
        preferred_element_type=jnp.float32,
    )
    numerator = numerator + jnp.einsum(
        "ckgij,cjkd->ckgid", fresh_weights, own_fresh[..., HD:], preferred_element_type=jnp.float32
    )
    result = numerator / denominator[..., None]
    flattened = jnp.transpose(result, (0, 3, 1, 2, 4)).reshape(
        cand_here, new_count * policy_heads * HD
    )
    placed = jnp.einsum(
        "cs,cx->sx", matched.astype(jnp.float32), flattened, precision=lax.Precision.HIGHEST
    )
    return lax.psum_scatter(
        placed.reshape(lane_number, new_count, policy_heads * HD).astype(jnp.bfloat16),
        "cand", scatter_dimension=0, tiled=True,
    )


def local(
    nz, nt,
    response_latest_embeddings,
    critic_probe_projector,
    critic_pair_projector,
    critic_stored_pairs,
    critic_grading_vector,
    actor_stored_pairs,
    filled_extents,
    kept_responses,
    actor_latest_probes,
    actor_latest_pairs,
):
    shares = reward_partial(
        nz, nt, response_latest_embeddings, critic_probe_projector, critic_pair_projector,
        critic_stored_pairs, critic_grading_vector,
    )
    token_rewards = lax.psum(jnp.sum(shares, axis=-1), "tensor")
    slot_rows = policy(
        response_latest_embeddings.shape[0], actor_stored_pairs, filled_extents, kept_responses,
        actor_latest_probes, actor_latest_pairs,
    )
    return (token_rewards, slot_rows)


def solution(mesh):
    placed = (
        P(("groups", "cand"), None, "tensor"),
        P("cand", "tensor"),
        P("cand", "tensor"),
        P(("groups", "cand"), None, "tensor"),
        P("tensor"),
        P(("groups", "cand"), None, "tensor", None),
        P("groups"),
        P("groups"),
        P(("groups", "cand"), None, "tensor"),
        P(("groups", "cand"), None, "tensor"),
    )
    return jax.shard_map(
        functools.partial(local, mesh.shape["cand"], mesh.shape["tensor"]),
        mesh=mesh,
        in_specs=placed,
        out_specs=(P(("groups", "cand"), None), P(("groups", "cand"), None, "tensor")),
        check_vma=False,
    )
```

```python
import functools

import jax
import jax.numpy as jnp
from jax import lax
from jax.experimental import pallas as pl
from jax.experimental.pallas import tpu as pltpu
from jax.sharding import PartitionSpec as P

HD = 128
CW = 2 * HD
AHEAD = 2
MESH = pl.DeviceIdType.MESH

masked_value = -1e30


def project_kernel(
    nz, nt, per_group,
    x_ref, wq_ref, wkv_ref, cache_ref, grade_ref, out_ref,
    xbuf, wbuf, cbuf, acts,
    load_sem, right_sem, left_sem, line_sem, pair_send, pair_recv,
    x_right, x_left, x_line, x_pair_send, x_pair_recv,
):
    nchunk, depth, _ = wbuf.shape
    dz = depth // nz
    half = dz // 2
    nx = nt // 2
    cands, span, _ = out_ref.shape
    context = cbuf.shape[1]
    qchunks = per_group * HD // CW
    stride = 1 + qchunks
    y = lax.axis_index("groups")
    z = lax.axis_index("cand")
    t = lax.axis_index("tensor")
    x = t // 2
    c = t - 2 * x

    loads = []
    for k in range(nchunk):
        g, j = k // stride, k % stride
        if j == 0:
            src = wkv_ref.at[:, pl.ds(g * CW, CW)]
        else:
            src = wq_ref.at[:, pl.ds((g * qchunks + j - 1) * CW, CW)]
        loads.append(
            pltpu.make_async_copy(
                src, wbuf.at[k, pl.ds(pl.multiple_of(z * dz, dz), dz), :], load_sem.at[k]
            )
        )
    x_load = pltpu.make_async_copy(x_ref, xbuf.at[t], load_sem.at[nchunk])
    c_load = pltpu.make_async_copy(cache_ref, cbuf, load_sem.at[nchunk + 1])
    for k in range(min(AHEAD, nchunk)):
        loads[k].start()
    x_load.start()
    for k in range(min(AHEAD, nchunk), nchunk):
        loads[k].start()
    c_load.start()

    barrier = pltpu.get_barrier_semaphore()

    def greet(device):
        pl.semaphore_signal(barrier, inc=1, device_id=device, device_id_type=MESH)

    greet({"groups": 1 - y})
    greet({"tensor": 2 * x + 1 - c})

    @pl.when(z > 0)
    def _():
        greet({"cand": z - 1})

    @pl.when(z < nz - 1)
    def _():
        greet({"cand": z + 1})

    @pl.when(x > 0)
    def _():
        greet({"tensor": t - 2})

    @pl.when(x < nx - 1)
    def _():
        greet({"tensor": t + 2})

    ends = [z > 0, z < nz - 1, x > 0, x < nx - 1]
    pl.semaphore_wait(barrier, 2 + sum(e.astype(jnp.int32) for e in ends))

    def remote(ref, send, recv, device):
        return pltpu.make_async_remote_copy(
            src_ref=ref, dst_ref=ref, send_sem=send, recv_sem=recv,
            device_id=device, device_id_type=MESH,
        )

    def piece(k, o, side):
        return wbuf.at[k, pl.ds(pl.multiple_of(o * dz + side * half, half), half), :]

    def go_right(k, o):
        return remote(piece(k, o, y), right_sem.at[k, o], line_sem.at[k, o], {"cand": z + 1})

    def go_left(k, o):
        return remote(piece(k, o, y), left_sem.at[k, o], line_sem.at[k, o], {"cand": z - 1})

    def to_pair(k, o):
        return remote(piece(k, o, y), pair_send.at[k, o], pair_recv.at[k, o], {"groups": 1 - y})

    def from_pair(k, o):
        return remote(piece(k, o, 1 - y), pair_send.at[k, o], pair_recv.at[k, o], {"groups": 1 - y})

    def send_own(k):
        @pl.when(z < nz - 1)
        def _():
            go_right(k, z).start()

        @pl.when(z > 0)
        def _():
            go_left(k, z).start()

    def x_go_right(o):
        return remote(xbuf.at[2 * o + c], x_right.at[o], x_line.at[o], {"tensor": t + 2})

    def x_go_left(o):
        return remote(xbuf.at[2 * o + c], x_left.at[o], x_line.at[o], {"tensor": t - 2})

    def x_to_pair(o):
        return remote(xbuf.at[2 * o + c], x_pair_send.at[o], x_pair_recv.at[o], {"tensor": 2 * x + 1 - c})

    def x_from_pair(o):
        return remote(xbuf.at[2 * o + 1 - c], x_pair_send.at[o], x_pair_recv.at[o], {"tensor": 2 * x + 1 - c})

    for k in range(min(AHEAD, nchunk)):
        loads[k].wait()
        send_own(k)
    x_load.wait()

    @pl.when(x < nx - 1)
    def _():
        x_go_right(x).start()

    @pl.when(x > 0)
    def _():
        x_go_left(x).start()

    x_to_pair(x).start()
    for k in range(min(AHEAD, nchunk), nchunk):
        loads[k].wait()
    c_load.wait()
    out_ref[...] = jnp.zeros_like(out_ref)

    def finish_x():
        for d in range(1, nx):
            @pl.when(x - d >= 0)
            def _(d=d):
                x_go_right(x - d).wait_recv()
                x_to_pair(x - d).start()

                @pl.when(x < nx - 1)
                def _():
                    x_go_right(x - d).start()

            @pl.when(x + d < nx)
            def _(d=d):
                x_go_left(x + d).wait_recv()
                x_to_pair(x + d).start()

                @pl.when(x > 0)
                def _():
                    x_go_left(x + d).start()

        for o in range(nx):
            x_from_pair(o).wait_recv()

    def relay(k, first, last):
        def one(d, carry):
            @pl.when(z - d >= 0)
            def _():
                o = z - d
                go_right(k, o).wait_recv()

                @pl.when(z < nz - 1)
                def _():
                    go_right(k, o).start()

                to_pair(k, o).start()

            @pl.when(z + d < nz)
            def _():
                o = z + d
                go_left(k, o).wait_recv()

                @pl.when(z > 0)
                def _():
                    go_left(k, o).start()

                to_pair(k, o).start()

            return carry

        lax.fori_loop(first, last, one, 0)

    rows = cands * span
    dx = depth // nt
    row_tile = rows // 3

    def attend(k):
        g = k // stride
        base = pl.multiple_of(g * CW, CW)
        kv_at = g * stride
        ri = lax.broadcasted_iota(jnp.int32, (span, span), 0)
        ci = lax.broadcasted_iota(jnp.int32, (span, span), 1)
        head0 = (g * qchunks + (k - kv_at) - 1) * 2

        def one(b, carry):
            at = pl.ds(pl.multiple_of(b * span, span), span)
            old_k = cbuf[b, :, pl.ds(base, HD)]
            old_v = cbuf[b, :, pl.ds(pl.multiple_of(base + HD, HD), HD)]
            new_k = acts[kv_at, at, :HD]
            new_v = acts[kv_at, at, HD:]
            for h in range(2):
                q = acts[k, at, h * HD:(h + 1) * HD]
                dims = (((1,), (1,)), ((), ()))
                s1 = lax.dot_general(q, old_k, dims, preferred_element_type=jnp.float32)
                s2 = lax.dot_general(q, new_k, dims, preferred_element_type=jnp.float32)
                s2 = jnp.where(ri >= ci, s2, masked_value)
                top = jnp.maximum(
                    jnp.max(s1, axis=1, keepdims=True), jnp.max(s2, axis=1, keepdims=True)
                )
                scale = HD ** -0.5
                e1 = jnp.exp((s1 - top) * scale)
                e2 = jnp.exp((s2 - top) * scale)
                total = jnp.sum(e1, axis=1, keepdims=True) + jnp.sum(e2, axis=1, keepdims=True)
                o = jnp.dot(e1.astype(jnp.bfloat16), old_v, preferred_element_type=jnp.float32)
                o = o + jnp.dot(e2.astype(jnp.bfloat16), new_v, preferred_element_type=jnp.float32)
                weight = grade_ref[pl.ds(head0 + h, 1), :]
                out_ref[b] += (o / total) * weight
            return carry

        lax.fori_loop(0, cands, one, 0)

    def compute(k):
        def take(d, carry):
            o = jnp.where(d < z, d, d + 1)
            from_pair(k, o).wait_recv()
            return carry

        lax.fori_loop(0, nz - 1, take, 0)

        def tile(r, carry):
            at = pl.ds(pl.multiple_of(r * row_tile, row_tile), row_tile)
            acc = jnp.zeros((row_tile, CW), jnp.float32)
            for s in range(nt):
                acc = acc + jnp.dot(
                    xbuf[s, at, :], wbuf[k, s * dx:(s + 1) * dx, :],
                    preferred_element_type=jnp.float32,
                )
            acts[k, at, :] = acc.astype(jnp.bfloat16)
            return carry

        lax.fori_loop(0, rows // row_tile, tile, 0)

        @pl.when(lax.rem(k, stride) != 0)
        def _():
            attend(k)

    def done(k):
        return jnp.where(k < 2, 0, k)

    def step(k, carry):
        @pl.when(k + AHEAD < nchunk)
        def _():
            send_own(k + AHEAD)

        relay(k, 1, 2)

        @pl.when(k == 2)
        def _():
            finish_x()

        def inner(j, c2):
            compute(j)
            return c2

        lax.fori_loop(done(k - 1), done(k), inner, 0)
        relay(k, 2, nz)
        return carry

    lax.fori_loop(0, nchunk, step, 0)
    lax.fori_loop(nchunk - 1, nchunk, lambda j, c2: (compute(j), c2)[1], 0)

    def drain(k, carry):
        def one(o, c2):
            @pl.when((o <= z) & (z < nz - 1))
            def _():
                go_right(k, o).wait_send()

            @pl.when((o >= z) & (z > 0))
            def _():
                go_left(k, o).wait_send()

            @pl.when(o != z)
            def _():
                to_pair(k, o).wait_send()

            return c2

        lax.fori_loop(0, nz, one, 0)
        return carry

    lax.fori_loop(0, nchunk, drain, 0)
    for o in range(nx):
        x_to_pair(o).wait_send()

        @pl.when((o <= x) & (x < nx - 1))
        def _(o=o):
            x_go_right(o).wait_send()

        @pl.when((o >= x) & (x > 0))
        def _(o=o):
            x_go_left(o).wait_send()


def reward_partial(nz, nt, x, wq, wkv, cache, grade):
    cands, span, dx = x.shape
    rows = cands * span
    depth = wq.shape[0] * nz
    groups_here = wkv.shape[1] // CW
    per_group = wq.shape[1] // HD // groups_here
    nchunk = (wq.shape[1] + wkv.shape[1]) // CW
    dma = pltpu.SemaphoreType.DMA
    nx = nt // 2
    anywhere = pl.BlockSpec(memory_space=pl.ANY)
    return pl.pallas_call(
        functools.partial(project_kernel, nz, nt, per_group),
        out_shape=jax.ShapeDtypeStruct((cands, span, HD), jnp.float32),
        in_specs=[anywhere] * 4 + [pl.BlockSpec(memory_space=pltpu.VMEM)],
        out_specs=pl.BlockSpec(memory_space=pltpu.VMEM),
        scratch_shapes=[
            pltpu.VMEM((nt, rows, dx), jnp.bfloat16),
            pltpu.VMEM((nchunk, depth, CW), jnp.bfloat16),
            pltpu.VMEM(cache.shape, jnp.bfloat16),
            pltpu.VMEM((nchunk, rows, CW), jnp.bfloat16),
            dma((nchunk + 2,)),
            dma((nchunk, nz)), dma((nchunk, nz)), dma((nchunk, nz)),
            dma((nchunk, nz)), dma((nchunk, nz)),
            dma((nx,)), dma((nx,)), dma((nx,)), dma((nx,)), dma((nx,)),
        ],
        compiler_params=pltpu.CompilerParams(
            collective_id=0, has_side_effects=True, vmem_limit_bytes=67043328
        ),
    )(x.reshape(rows, dx), wq, wkv, cache, grade.reshape(-1, HD))


def policy(
    cand_here, actor_stored_pairs, filled_extents, kept_responses, actor_latest_probes, actor_latest_pairs
):
    key_scale = HD ** (-0.5)
    device_here = lax.axis_index("cand")
    lane_number = kept_responses.shape[0]
    new_count = actor_latest_probes.shape[1]
    kv_here = actor_stored_pairs.shape[2]
    policy_heads = actor_latest_probes.shape[2] // HD
    policy_group = policy_heads // kv_here
    cache_len = actor_stored_pairs.shape[1]
    causal_new = lax.broadcasted_iota(jnp.int32, (new_count, new_count), 0) >= lax.broadcasted_iota(
        jnp.int32, (new_count, new_count), 1
    )
    both = lax.all_gather(
        jnp.concatenate([actor_latest_probes, actor_latest_pairs], axis=2), "cand", axis=0, tiled=True
    )
    all_queries = both[..., : policy_heads * HD]
    all_fresh = both[..., policy_heads * HD:]
    ids_here = device_here * cand_here + lax.broadcasted_iota(jnp.int32, (cand_here,), 0)
    matched = kept_responses[None, :] == ids_here[:, None]
    slot_index = jnp.sum(
        jnp.where(matched, lax.broadcasted_iota(jnp.int32, (cand_here, lane_number), 1), 0), axis=1
    )
    own_queries = jnp.take(all_queries, slot_index, axis=0).reshape(
        cand_here, new_count, kv_here, policy_group, HD
    )
    own_fresh = jnp.take(all_fresh, slot_index, axis=0).reshape(
        cand_here, new_count, kv_here, 2 * HD
    )
    sequence_places = lax.broadcasted_iota(jnp.int32, (cache_len,), 0)
    living = sequence_places[None, :] < jnp.take(filled_extents, ids_here)[:, None]
    living = living[:, None, None, None, :]
    scores = (
        jnp.einsum(
            "cikgd,ctkd->ckgit", own_queries, actor_stored_pairs[..., :HD],
            preferred_element_type=jnp.float32,
        )
        * key_scale
    )
    scores = jnp.where(living, scores, masked_value)
    fresh_scores = (
        jnp.einsum(
            "cikgd,cjkd->ckgij", own_queries, own_fresh[..., :HD], preferred_element_type=jnp.float32
        )
        * key_scale
    )
    fresh_scores = jnp.where(causal_new, fresh_scores, masked_value)
    peak = jnp.maximum(jnp.max(scores, axis=-1), jnp.max(fresh_scores, axis=-1))
    old_weights = jnp.where(living, jnp.exp(scores - peak[..., None]), 0.0)
    fresh_weights = jnp.where(causal_new, jnp.exp(fresh_scores - peak[..., None]), 0.0)
    denominator = jnp.sum(old_weights, axis=-1) + jnp.sum(fresh_weights, axis=-1)
    numerator = jnp.einsum(
        "ckgit,ctkd->ckgid", old_weights, actor_stored_pairs[..., HD:],
        preferred_element_type=jnp.float32,
    )
    numerator = numerator + jnp.einsum(
        "ckgij,cjkd->ckgid", fresh_weights, own_fresh[..., HD:], preferred_element_type=jnp.float32
    )
    result = numerator / denominator[..., None]
    flattened = jnp.transpose(result, (0, 3, 1, 2, 4)).reshape(
        cand_here, new_count * policy_heads * HD
    )
    placed = jnp.einsum(
        "cs,cx->sx", matched.astype(jnp.float32), flattened, precision=lax.Precision.HIGHEST
    )
    return lax.psum_scatter(
        placed.reshape(lane_number, new_count, policy_heads * HD).astype(jnp.bfloat16),
        "cand", scatter_dimension=0, tiled=True,
    )


def local(
    nz, nt,
    response_latest_embeddings,
    critic_probe_projector,
    critic_pair_projector,
    critic_stored_pairs,
    critic_grading_vector,
    actor_stored_pairs,
    filled_extents,
    kept_responses,
    actor_latest_probes,
    actor_latest_pairs,
):
    shares = reward_partial(
        nz, nt, response_latest_embeddings, critic_probe_projector, critic_pair_projector,
        critic_stored_pairs, critic_grading_vector,
    )
    token_rewards = lax.psum(jnp.sum(shares, axis=-1), "tensor")
    slot_rows = policy(
        response_latest_embeddings.shape[0], actor_stored_pairs, filled_extents, kept_responses,
        actor_latest_probes, actor_latest_pairs,
    )
    return (token_rewards, slot_rows)


def solution(mesh):
    placed = (
        P(("groups", "cand"), None, "tensor"),
        P("cand", "tensor"),
        P("cand", "tensor"),
        P(("groups", "cand"), None, "tensor"),
        P("tensor"),
        P(("groups", "cand"), None, "tensor", None),
        P("groups"),
        P("groups"),
        P(("groups", "cand"), None, "tensor"),
        P(("groups", "cand"), None, "tensor"),
    )
    return jax.shard_map(
        functools.partial(local, mesh.shape["cand"], mesh.shape["tensor"]),
        mesh=mesh,
        in_specs=placed,
        out_specs=(P(("groups", "cand"), None), P(("groups", "cand"), None, "tensor")),
        check_vma=False,
    )
```

```python
import functools

import jax
import jax.numpy as jnp
from jax import lax
from jax.experimental import pallas as pl
from jax.experimental.pallas import tpu as pltpu
from jax.sharding import PartitionSpec as P

HD = 128
CW = 2 * HD
AHEAD = 2
MESH = pl.DeviceIdType.MESH

masked_value = -1e30


def project_kernel(
    nz, nt, per_group,
    x_ref, wq_ref, wkv_ref, cache_ref, grade_ref, slots_ref, out_ref, mine_ref,
    xbuf, wbuf, cbuf, acts,
    load_sem, right_sem, left_sem, line_sem, pair_send, pair_recv,
    x_right, x_left, x_line, x_pair_send, x_pair_recv,
    given, give_send, give_recv,
):
    nchunk, depth, _ = wbuf.shape
    dz = depth // nz
    half = dz // 2
    nx = nt // 2
    cands, span, _ = out_ref.shape
    context = cbuf.shape[1]
    qchunks = per_group * HD // CW
    stride = 1 + qchunks
    y = lax.axis_index("groups")
    z = lax.axis_index("cand")
    t = lax.axis_index("tensor")
    x = t // 2
    c = t - 2 * x

    loads = []
    for k in range(nchunk):
        g, j = k // stride, k % stride
        if j == 0:
            src = wkv_ref.at[:, pl.ds(g * CW, CW)]
        else:
            src = wq_ref.at[:, pl.ds((g * qchunks + j - 1) * CW, CW)]
        loads.append(
            pltpu.make_async_copy(
                src, wbuf.at[k, pl.ds(pl.multiple_of(z * dz, dz), dz), :], load_sem.at[k]
            )
        )
    x_load = pltpu.make_async_copy(x_ref, xbuf.at[t], load_sem.at[nchunk])
    c_load = pltpu.make_async_copy(cache_ref, cbuf, load_sem.at[nchunk + 1])
    for k in range(min(AHEAD, nchunk)):
        loads[k].start()
    x_load.start()
    for k in range(min(AHEAD, nchunk), nchunk):
        loads[k].start()
    c_load.start()

    barrier = pltpu.get_barrier_semaphore()

    def greet(device):
        pl.semaphore_signal(barrier, inc=1, device_id=device, device_id_type=MESH)

    greet({"groups": 1 - y})
    greet({"tensor": 2 * x + 1 - c})

    def greet_peer(d, carry):
        greet({"cand": lax.rem(z + d, nz)})
        return carry

    lax.fori_loop(1, nz, greet_peer, 0)

    @pl.when(x > 0)
    def _():
        greet({"tensor": t - 2})

    @pl.when(x < nx - 1)
    def _():
        greet({"tensor": t + 2})

    ends = [x > 0, x < nx - 1]
    pl.semaphore_wait(barrier, nz + 1 + sum(e.astype(jnp.int32) for e in ends))

    def remote(ref, send, recv, device):
        return pltpu.make_async_remote_copy(
            src_ref=ref, dst_ref=ref, send_sem=send, recv_sem=recv,
            device_id=device, device_id_type=MESH,
        )

    def piece(k, o, side):
        return wbuf.at[k, pl.ds(pl.multiple_of(o * dz + side * half, half), half), :]

    def go_right(k, o):
        return remote(piece(k, o, y), right_sem.at[k, o], line_sem.at[k, o], {"cand": z + 1})

    def go_left(k, o):
        return remote(piece(k, o, y), left_sem.at[k, o], line_sem.at[k, o], {"cand": z - 1})

    def to_pair(k, o):
        return remote(piece(k, o, y), pair_send.at[k, o], pair_recv.at[k, o], {"groups": 1 - y})

    def from_pair(k, o):
        return remote(piece(k, o, 1 - y), pair_send.at[k, o], pair_recv.at[k, o], {"groups": 1 - y})

    def send_own(k):
        @pl.when(z < nz - 1)
        def _():
            go_right(k, z).start()

        @pl.when(z > 0)
        def _():
            go_left(k, z).start()

    def give(o):
        return pltpu.make_async_remote_copy(
            src_ref=slots_ref.at[o], dst_ref=given.at[z], send_sem=give_send.at[o],
            recv_sem=give_recv.at[z], device_id={"cand": o}, device_id_type=MESH,
        )

    def get(o):
        return pltpu.make_async_remote_copy(
            src_ref=slots_ref.at[o], dst_ref=given.at[o], send_sem=give_send.at[o],
            recv_sem=give_recv.at[o], device_id={"cand": o}, device_id_type=MESH,
        )

    def x_go_right(o):
        return remote(xbuf.at[2 * o + c], x_right.at[o], x_line.at[o], {"tensor": t + 2})

    def x_go_left(o):
        return remote(xbuf.at[2 * o + c], x_left.at[o], x_line.at[o], {"tensor": t - 2})

    def x_to_pair(o):
        return remote(xbuf.at[2 * o + c], x_pair_send.at[o], x_pair_recv.at[o], {"tensor": 2 * x + 1 - c})

    def x_from_pair(o):
        return remote(xbuf.at[2 * o + 1 - c], x_pair_send.at[o], x_pair_recv.at[o], {"tensor": 2 * x + 1 - c})

    def give_one(d, carry):
        give(lax.rem(z + d, nz)).start()
        return carry

    lax.fori_loop(1, nz, give_one, 0)
    for k in range(min(AHEAD, nchunk)):
        loads[k].wait()
        send_own(k)
    x_load.wait()

    @pl.when(x < nx - 1)
    def _():
        x_go_right(x).start()

    @pl.when(x > 0)
    def _():
        x_go_left(x).start()

    x_to_pair(x).start()
    for k in range(min(AHEAD, nchunk), nchunk):
        loads[k].wait()
    c_load.wait()
    out_ref[...] = jnp.zeros_like(out_ref)

    def finish_x():
        for d in range(1, nx):
            @pl.when(x - d >= 0)
            def _(d=d):
                x_go_right(x - d).wait_recv()
                x_to_pair(x - d).start()

                @pl.when(x < nx - 1)
                def _():
                    x_go_right(x - d).start()

            @pl.when(x + d < nx)
            def _(d=d):
                x_go_left(x + d).wait_recv()
                x_to_pair(x + d).start()

                @pl.when(x > 0)
                def _():
                    x_go_left(x + d).start()

        for o in range(nx):
            x_from_pair(o).wait_recv()

    def relay(k, first, last):
        def one(d, carry):
            @pl.when(z - d >= 0)
            def _():
                o = z - d
                go_right(k, o).wait_recv()

                @pl.when(z < nz - 1)
                def _():
                    go_right(k, o).start()

                to_pair(k, o).start()

            @pl.when(z + d < nz)
            def _():
                o = z + d
                go_left(k, o).wait_recv()

                @pl.when(z > 0)
                def _():
                    go_left(k, o).start()

                to_pair(k, o).start()

            return carry

        lax.fori_loop(first, last, one, 0)

    rows = cands * span
    dx = depth // nt
    row_tile = rows // 3

    def attend(k):
        g = k // stride
        base = pl.multiple_of(g * CW, CW)
        kv_at = g * stride
        ri = lax.broadcasted_iota(jnp.int32, (span, span), 0)
        ci = lax.broadcasted_iota(jnp.int32, (span, span), 1)
        head0 = (g * qchunks + (k - kv_at) - 1) * 2

        def one(b, carry):
            at = pl.ds(pl.multiple_of(b * span, span), span)
            old_k = cbuf[b, :, pl.ds(base, HD)]
            old_v = cbuf[b, :, pl.ds(pl.multiple_of(base + HD, HD), HD)]
            new_k = acts[kv_at, at, :HD]
            new_v = acts[kv_at, at, HD:]
            for h in range(2):
                q = acts[k, at, h * HD:(h + 1) * HD]
                dims = (((1,), (1,)), ((), ()))
                s1 = lax.dot_general(q, old_k, dims, preferred_element_type=jnp.float32)
                s2 = lax.dot_general(q, new_k, dims, preferred_element_type=jnp.float32)
                s2 = jnp.where(ri >= ci, s2, masked_value)
                top = jnp.maximum(
                    jnp.max(s1, axis=1, keepdims=True), jnp.max(s2, axis=1, keepdims=True)
                )
                scale = HD ** -0.5
                e1 = jnp.exp((s1 - top) * scale)
                e2 = jnp.exp((s2 - top) * scale)
                total = jnp.sum(e1, axis=1, keepdims=True) + jnp.sum(e2, axis=1, keepdims=True)
                o = jnp.dot(e1.astype(jnp.bfloat16), old_v, preferred_element_type=jnp.float32)
                o = o + jnp.dot(e2.astype(jnp.bfloat16), new_v, preferred_element_type=jnp.float32)
                weight = grade_ref[pl.ds(head0 + h, 1), :]
                out_ref[b] += (o / total) * weight
            return carry

        lax.fori_loop(0, cands, one, 0)

    def project(k):
        def take(d, carry):
            o = jnp.where(d < z, d, d + 1)
            from_pair(k, o).wait_recv()
            return carry

        lax.fori_loop(0, nz - 1, take, 0)

        def tile(r, carry):
            at = pl.ds(pl.multiple_of(r * row_tile, row_tile), row_tile)
            acc = jnp.zeros((row_tile, CW), jnp.float32)
            for s in range(nt):
                acc = acc + jnp.dot(
                    xbuf[s, at, :], wbuf[k, s * dx:(s + 1) * dx, :],
                    preferred_element_type=jnp.float32,
                )
            acts[k, at, :] = acc.astype(jnp.bfloat16)
            return carry

        lax.fori_loop(0, rows // row_tile, tile, 0)

    def units(first, last, unit):
        def one(j, carry):
            unit(j)
            return carry

        lax.fori_loop(first, last, one, 0)

    def attend_if(k):
        @pl.when(lax.rem(k, stride) != 0)
        def _():
            attend(k)

    def step(k, carry):
        @pl.when(k + AHEAD < nchunk)
        def _():
            send_own(k + AHEAD)

        relay(k, 1, 2)

        @pl.when(k == 2)
        def _():
            finish_x()

        @pl.when(k >= 2)
        def _():
            project(jnp.where(k == 2, 0, k - 1))

        relay(k, 2, min(3, nz))

        @pl.when(k == 2)
        def _():
            project(k - 1)

        @pl.when(k >= 2)
        def _():
            attend_if(k - 1)

        relay(k, 3, nz)
        return carry

    lax.fori_loop(0, nchunk, step, 0)
    units(nchunk - 1, nchunk, project)
    units(nchunk - 1, nchunk, attend_if)
    mine_ref[...] = slots_ref[z].astype(jnp.float32)

    def get_one(d, carry):
        o = lax.rem(z + d, nz)
        get(o).wait_recv()
        mine_ref[...] += given[o].astype(jnp.float32)
        give(o).wait_send()
        return carry

    lax.fori_loop(1, nz, get_one, 0)

    def drain(k, carry):
        def one(o, c2):
            @pl.when((o <= z) & (z < nz - 1))
            def _():
                go_right(k, o).wait_send()

            @pl.when((o >= z) & (z > 0))
            def _():
                go_left(k, o).wait_send()

            @pl.when(o != z)
            def _():
                to_pair(k, o).wait_send()

            return c2

        lax.fori_loop(0, nz, one, 0)
        return carry

    lax.fori_loop(0, nchunk, drain, 0)
    for o in range(nx):
        x_to_pair(o).wait_send()

        @pl.when((o <= x) & (x < nx - 1))
        def _(o=o):
            x_go_right(o).wait_send()

        @pl.when((o >= x) & (x > 0))
        def _(o=o):
            x_go_left(o).wait_send()


def reward_partial(nz, nt, x, wq, wkv, cache, grade, slots):
    cands, span, dx = x.shape
    rows = cands * span
    depth = wq.shape[0] * nz
    groups_here = wkv.shape[1] // CW
    per_group = wq.shape[1] // HD // groups_here
    nchunk = (wq.shape[1] + wkv.shape[1]) // CW
    dma = pltpu.SemaphoreType.DMA
    nx = nt // 2
    anywhere = pl.BlockSpec(memory_space=pl.ANY)
    return pl.pallas_call(
        functools.partial(project_kernel, nz, nt, per_group),
        out_shape=(
            jax.ShapeDtypeStruct((cands, span, HD), jnp.float32),
            jax.ShapeDtypeStruct(slots.shape[1:], jnp.float32),
        ),
        in_specs=[anywhere] * 4 + [pl.BlockSpec(memory_space=pltpu.VMEM)] * 2,
        out_specs=(pl.BlockSpec(memory_space=pltpu.VMEM),) * 2,
        scratch_shapes=[
            pltpu.VMEM((nt, rows, dx), jnp.bfloat16),
            pltpu.VMEM((nchunk, depth, CW), jnp.bfloat16),
            pltpu.VMEM(cache.shape, jnp.bfloat16),
            pltpu.VMEM((nchunk, rows, CW), jnp.bfloat16),
            dma((nchunk + 2,)),
            dma((nchunk, nz)), dma((nchunk, nz)), dma((nchunk, nz)),
            dma((nchunk, nz)), dma((nchunk, nz)),
            dma((nx,)), dma((nx,)), dma((nx,)), dma((nx,)), dma((nx,)),
            pltpu.VMEM(slots.shape, jnp.bfloat16), dma((nz,)), dma((nz,)),
        ],
        compiler_params=pltpu.CompilerParams(
            collective_id=0, has_side_effects=True, vmem_limit_bytes=67043328
        ),
    )(x.reshape(rows, dx), wq, wkv, cache, grade.reshape(-1, HD), slots)


def gather_kernel(nz, own_ref, out_ref, buf, send, recv):
    z = lax.axis_index("cand")
    barrier = pltpu.get_barrier_semaphore()

    def greet(d, carry):
        pl.semaphore_signal(
            barrier, inc=1, device_id={"cand": lax.rem(z + d, nz)}, device_id_type=MESH
        )
        return carry

    lax.fori_loop(1, nz, greet, 0)
    pl.semaphore_wait(barrier, nz - 1)

    def copy(o, lands):
        return pltpu.make_async_remote_copy(
            src_ref=own_ref, dst_ref=buf.at[lands], send_sem=send.at[o],
            recv_sem=recv.at[lands], device_id={"cand": o}, device_id_type=MESH,
        )

    def start(d, carry):
        copy(lax.rem(z + d, nz), z).start()
        return carry

    lax.fori_loop(1, nz, start, 0)
    out_ref[z] = own_ref[...]

    def finish(d, carry):
        o = lax.rem(z + d, nz)
        copy(o, o).wait_recv()
        out_ref[o] = buf[o]
        copy(o, z).wait_send()
        return carry

    lax.fori_loop(1, nz, finish, 0)


def gather_slots(nz, own):
    lanes, count, width = own.shape
    flat = own.reshape(lanes * count, width)
    vmem = pl.BlockSpec(memory_space=pltpu.VMEM)
    whole = pl.pallas_call(
        functools.partial(gather_kernel, nz),
        out_shape=jax.ShapeDtypeStruct((nz,) + flat.shape, own.dtype),
        in_specs=[vmem],
        out_specs=vmem,
        scratch_shapes=[
            pltpu.VMEM((nz,) + flat.shape, own.dtype),
            pltpu.SemaphoreType.DMA((nz,)), pltpu.SemaphoreType.DMA((nz,)),
        ],
        compiler_params=pltpu.CompilerParams(
            collective_id=1, has_side_effects=True, vmem_limit_bytes=1 << 22
        ),
    )(flat)
    return whole.reshape(nz * lanes, count, width)


def policy(
    nz, cand_here, actor_stored_pairs, filled_extents, kept_responses, actor_latest_probes, actor_latest_pairs
):
    key_scale = HD ** (-0.5)
    device_here = lax.axis_index("cand")
    lane_number = kept_responses.shape[0]
    new_count = actor_latest_probes.shape[1]
    kv_here = actor_stored_pairs.shape[2]
    policy_heads = actor_latest_probes.shape[2] // HD
    policy_group = policy_heads // kv_here
    cache_len = actor_stored_pairs.shape[1]
    causal_new = lax.broadcasted_iota(jnp.int32, (new_count, new_count), 0) >= lax.broadcasted_iota(
        jnp.int32, (new_count, new_count), 1
    )
    both = gather_slots(
        nz, jnp.concatenate([actor_latest_probes, actor_latest_pairs], axis=2)
    )
    all_queries = both[..., : policy_heads * HD]
    all_fresh = both[..., policy_heads * HD:]
    ids_here = device_here * cand_here + lax.broadcasted_iota(jnp.int32, (cand_here,), 0)
    matched = kept_responses[None, :] == ids_here[:, None]
    slot_index = jnp.sum(
        jnp.where(matched, lax.broadcasted_iota(jnp.int32, (cand_here, lane_number), 1), 0), axis=1
    )
    own_queries = jnp.take(all_queries, slot_index, axis=0).reshape(
        cand_here, new_count, kv_here, policy_group, HD
    )
    own_fresh = jnp.take(all_fresh, slot_index, axis=0).reshape(
        cand_here, new_count, kv_here, 2 * HD
    )
    sequence_places = lax.broadcasted_iota(jnp.int32, (cache_len,), 0)
    living = sequence_places[None, :] < jnp.take(filled_extents, ids_here)[:, None]
    living = living[:, None, None, None, :]
    scores = (
        jnp.einsum(
            "cikgd,ctkd->ckgit", own_queries, actor_stored_pairs[..., :HD],
            preferred_element_type=jnp.float32,
        )
        * key_scale
    )
    scores = jnp.where(living, scores, masked_value)
    fresh_scores = (
        jnp.einsum(
            "cikgd,cjkd->ckgij", own_queries, own_fresh[..., :HD], preferred_element_type=jnp.float32
        )
        * key_scale
    )
    fresh_scores = jnp.where(causal_new, fresh_scores, masked_value)
    peak = jnp.maximum(jnp.max(scores, axis=-1), jnp.max(fresh_scores, axis=-1))
    old_weights = jnp.where(living, jnp.exp(scores - peak[..., None]), 0.0)
    fresh_weights = jnp.where(causal_new, jnp.exp(fresh_scores - peak[..., None]), 0.0)
    denominator = jnp.sum(old_weights, axis=-1) + jnp.sum(fresh_weights, axis=-1)
    numerator = jnp.einsum(
        "ckgit,ctkd->ckgid", old_weights, actor_stored_pairs[..., HD:],
        preferred_element_type=jnp.float32,
    )
    numerator = numerator + jnp.einsum(
        "ckgij,cjkd->ckgid", fresh_weights, own_fresh[..., HD:], preferred_element_type=jnp.float32
    )
    result = numerator / denominator[..., None]
    flattened = jnp.transpose(result, (0, 3, 1, 2, 4)).reshape(
        cand_here, new_count * policy_heads * HD
    )
    placed = jnp.einsum(
        "cs,cx->sx", matched.astype(jnp.float32), flattened, precision=lax.Precision.HIGHEST
    )
    return placed.reshape(nz, lane_number // nz * new_count, policy_heads * HD).astype(jnp.bfloat16)


def local(
    nz, nt,
    response_latest_embeddings,
    critic_probe_projector,
    critic_pair_projector,
    critic_stored_pairs,
    critic_grading_vector,
    actor_stored_pairs,
    filled_extents,
    kept_responses,
    actor_latest_probes,
    actor_latest_pairs,
):
    slots = policy(
        nz, response_latest_embeddings.shape[0], actor_stored_pairs, filled_extents, kept_responses,
        actor_latest_probes, actor_latest_pairs,
    )
    shares, mine = reward_partial(
        nz, nt, response_latest_embeddings, critic_probe_projector, critic_pair_projector,
        critic_stored_pairs, critic_grading_vector, slots,
    )
    token_rewards = lax.psum(jnp.sum(shares, axis=-1), "tensor")
    slot_rows = mine.reshape(actor_latest_probes.shape).astype(jnp.bfloat16)
    return (token_rewards, slot_rows)


def solution(mesh):
    placed = (
        P(("groups", "cand"), None, "tensor"),
        P("cand", "tensor"),
        P("cand", "tensor"),
        P(("groups", "cand"), None, "tensor"),
        P("tensor"),
        P(("groups", "cand"), None, "tensor", None),
        P("groups"),
        P("groups"),
        P(("groups", "cand"), None, "tensor"),
        P(("groups", "cand"), None, "tensor"),
    )
    return jax.shard_map(
        functools.partial(local, mesh.shape["cand"], mesh.shape["tensor"]),
        mesh=mesh,
        in_specs=placed,
        out_specs=(P(("groups", "cand"), None), P(("groups", "cand"), None, "tensor")),
        check_vma=False,
    )
```
